32 devices in a mesh: dp: 8 (over z, y), mp: 4 (over x, core).
Axes of the slice: x: 2, y: 2, z: 4, core: 2. Of those that a mesh axis runs over, the one named last changes fastest.
Arguments:
- latents: bfloat16 [16, 24, 24, 1536], P('dp', 'mp'), may hold values from -6 to 6
- depth_kernel: bfloat16 [3, 3, 1536], replicated, may hold values from -2 to 2
- depth_bias: bfloat16 [1536], replicated, may hold values from -3 to 3
- expand_weight: bfloat16 [1536, 6144], P(None, 'mp'), may hold values from -2 to 2
- expand_bias: bfloat16 [6144], P('mp'), may hold values from -3 to 3
- response_gain: bfloat16 [6144], P('mp'), may hold values from -3 to 3
- response_bias: bfloat16 [6144], P('mp'), may hold values from -3 to 3
- shrink_weight: bfloat16 [6144, 1536], P('mp'), may hold values from -0.078125 to 0.078125
- shrink_bias: bfloat16 [1536], replicated, may hold values from -3 to 3
- time_embed: float32 [16, 192], P('dp'), may hold values from -6 to 6
- time_weight: bfloat16 [192, 3072], replicated, may hold values from -0.21875 to 0.21875
- time_bias: bfloat16 [3072], replicated, may hold values from -2 to 2
- caption: bfloat16 [16, 77, 1280], P('dp'), may hold values from -6 to 6
- drop_flags: int32 [16], P('dp'), may hold values 0 or 1
- caption_lengths: int32 [16], P('dp'), may hold values from 5 to 77
- text_weight: bfloat16 [1280, 1536], P(None, 'mp'), may hold values from -0.15625 to 0.15625
- text_bias: bfloat16 [1536], P('mp'), may hold values from -3 to 3
- project_weight: bfloat16 [1536, 3, 1536], P(None, None, 'mp'), may hold values from -0.15625 to 0.15625
- query_bias: bfloat16 [1536], P('mp'), may hold values from -2 to 2
- value_bias: bfloat16 [1536], P('mp'), may hold values from -2 to 2
- output_weight: bfloat16 [1536, 1536], P('mp'), may hold values from -1.25 to 1.25
- output_bias: bfloat16 [1536], replicated, may hold values from -3 to 3
- cotangent: bfloat16 [16, 24, 24, 1536], P('dp', 'mp'), may hold values from -6 to 6
Outputs:
- result: bfloat16 [16, 24, 24, 1536], P('dp', 'mp')
- latents_grad: bfloat16 [16, 24, 24, 1536], P('dp', 'mp')
- depth_kernel_grad: float32 [3, 3, 1536], P(None, None, ('dp', 'mp'))
- depth_bias_grad: float32 [1536], P(('dp', 'mp'))
- expand_weight_grad: float32 [1536, 6144], P('dp', 'mp')
- expand_bias_grad: float32 [6144], P(('mp', 'dp'))
- response_gain_grad: float32 [6144], P(('mp', 'dp'))
- response_bias_grad: float32 [6144], P(('mp', 'dp'))
- shrink_weight_grad: float32 [6144, 1536], P('mp', 'dp')
- shrink_bias_grad: float32 [1536], P('dp')
- time_weight_grad: float32 [192, 3072], P(None, 'dp')
- time_bias_grad: float32 [3072], P('dp')
- text_weight_grad: float32 [1280, 1536], P('dp', 'mp')
- text_bias_grad: float32 [1536], P(('mp', 'dp'))
- project_weight_grad: float32 [1536, 3, 1536], P('dp', None, 'mp')
- query_bias_grad: float32 [1536], P(('mp', 'dp'))
- value_bias_grad: float32 [1536], P(('mp', 'dp'))
- output_weight_grad: float32 [1536, 1536], P('mp', 'dp')
- output_bias_grad: float32 [1536], P('dp')
The draws below stay inside these ranges and needn't reach their ends.
All inputs are finite; a program needn't handle non-finite values. No bound on the sum of `drop_flags` on one device may be relied on, other than what follows from the above.
Results may differ from the reference program's by a relative error of at most 0.017.
Values may be sent and summed in bfloat16 or wider, within the bound.
A program may use at most 256 MiB of HBM per device.

```python
import math
import jax
import jax.numpy as jnp
from jax import lax

C = 1536
HEADS = 24
HEAD = 64
FF = 6144
CLIP = 1280
TDIM = 192
TEXT = 77
H = 24
W = 24
ITEMS = 16


def draw_expand_weight(key, part):
    key_base, key_rough = jax.random.split(jax.random.fold_in(key, 11))
    position = jnp.arange(FF, dtype=jnp.float32) / FF
    rising = jnp.exp(position * math.log(3.0))
    base = jax.random.truncated_normal(key_base, -4.0, 4.0, (C, FF), jnp.float32)
    rough = jnp.exp(jax.random.uniform(key_rough, (FF,), jnp.float32) * math.log(3.3))
    column_scale = rising * rough * (0.4 / math.sqrt(C))
    return (base * column_scale[None, :]).astype(jnp.bfloat16)


def touch_ends(values, stream_key, low, top_value):
    extent = values.shape
    index_at = [jax.random.randint(jax.random.fold_in(stream_key, axis), (), 0, extent[axis]) for axis in range(len(extent))]
    values = values.at[tuple(index_at)].set(low)
    longest = extent.index(max(extent))
    index_at[longest] = (index_at[longest] + 1) % extent[longest]
    return values.at[tuple(index_at)].set(top_value)


def levels(stream_key, shape, shards, least, top_value):
    gain = 1.0
    for dim, shards_of in shards:
        steps = jax.random.uniform(jax.random.fold_in(jax.random.fold_in(stream_key, 6), dim), (shards_of,), jnp.float32, least / len(shards), top_value / len(shards))
        gain = gain * jnp.repeat(jnp.exp(steps), shape[dim] // shards_of).reshape((-1,) + (1,) * (len(shape) - 1 - dim))
    return gain


def noise(key, shape, deviation, limit, pieces=(), held_as=jnp.bfloat16):
    values = deviation * jax.random.normal(key, shape, jnp.float32)
    if pieces:
        values = values * levels(key, shape, pieces, -0.22, 0.18)
    return jnp.clip(values, -limit, limit).astype(held_as)


def setup_inputs(seed: int = 0) -> dict:
    arg_keys = jax.random.split(jax.random.key(seed), 24)
    latents = noise(arg_keys[0], (ITEMS, H, W, C), 1.0, 6.0, ((0, 8), (1, 4)))
    depth_kernel = noise(arg_keys[1], (3, 3, C), 9 ** -0.5, 2.0)
    depth_bias = noise(arg_keys[2], (C,), 0.5, 3.0)
    expand_weight = draw_expand_weight(jax.random.fold_in(arg_keys[23], 71), 0)
    expand_bias = noise(arg_keys[4], (FF,), 0.5, 3.0, ((0, 4),))
    response_gain = noise(arg_keys[5], (FF,), 0.5, 3.0, ((0, 4),))
    response_bias = noise(arg_keys[6], (FF,), 0.5, 3.0, ((0, 4),))
    shrink_weight = noise(arg_keys[7], (FF, C), FF ** -0.5, 0.078125, ((0, 4),))
    shrink_bias = noise(arg_keys[8], (C,), 0.5, 3.0)
    time_embed = noise(arg_keys[9], (ITEMS, TDIM), 1.0, 6.0, ((0, 8),), jnp.float32)
    time_weight = noise(arg_keys[10], (TDIM, 2 * C), (4 * TDIM) ** -0.5, 0.21875)
    time_bias = noise(arg_keys[11], (2 * C,), 0.3, 2.0)
    caption = noise(arg_keys[12], (ITEMS, TEXT, CLIP), 1.0, 6.0, ((0, 8),))
    drop_flags = touch_ends((jax.random.randint(arg_keys[13], (ITEMS,), 0, 4) < 1).astype(jnp.int32), jax.random.fold_in(arg_keys[13], 1), 0, 1)
    caption_lengths = touch_ends(jax.random.randint(arg_keys[14], (ITEMS,), 5, TEXT + 1), jax.random.fold_in(arg_keys[14], 1), 5, TEXT).astype(jnp.int32)
    text_weight = noise(arg_keys[15], (CLIP, C), CLIP ** -0.5, 0.15625, ((1, 4),))
    text_bias = noise(arg_keys[16], (C,), 0.5, 3.0, ((0, 4),))
    project_weight = noise(arg_keys[17], (C, 3, C), C ** -0.5, 0.15625, ((2, 4),))
    query_bias = noise(arg_keys[18], (C,), 0.3, 2.0, ((0, 4),))
    value_bias = noise(arg_keys[19], (C,), 0.3, 2.0, ((0, 4),))
    output_weight = noise(arg_keys[20], (C, C), (C // 64) ** -0.5, 1.25, ((0, 4),))
    output_bias = noise(arg_keys[21], (C,), 0.5, 3.0)
    cotangent = noise(arg_keys[22], (ITEMS, H, W, C), 1.0, 6.0, ((0, 8), (1, 4)))
    return dict(latents=latents, depth_kernel=depth_kernel, depth_bias=depth_bias, expand_weight=expand_weight, expand_bias=expand_bias, response_gain=response_gain, response_bias=response_bias, shrink_weight=shrink_weight, shrink_bias=shrink_bias, time_embed=time_embed, time_weight=time_weight, time_bias=time_bias, caption=caption, drop_flags=drop_flags, caption_lengths=caption_lengths, text_weight=text_weight, text_bias=text_bias, project_weight=project_weight, query_bias=query_bias, value_bias=value_bias, output_weight=output_weight, output_bias=output_bias, cotangent=cotangent)


highest_mode = lax.Precision.HIGHEST

@jax.custom_vjp
def low(v):
    return lax.optimization_barrier(v.astype(jnp.bfloat16)).astype(jnp.float32)

@jax.custom_vjp
def low_back(v):
    return v

def low_keep(v):
    return (low(v), None)

def low_pass(kept, grad):
    return (grad,)

def back_keep(v):
    return (v, None)

def back_low(kept, grad):
    return (low(grad),)
low.defvjp(low_keep, low_pass)
low_back.defvjp(back_keep, back_low)

def layer_norm(values):
    centred = values - lax.optimization_barrier(jnp.mean(values, axis=-1, keepdims=True))
    return centred * lax.rsqrt(lax.optimization_barrier(jnp.mean(centred * centred, axis=-1, keepdims=True)) + 1e-06)

def item_forward(weights, latent, embedding, caption_item, drop_item, length_item):
    kernel, depth_bias, expand_weight, expand_bias, response_gain, response_bias, shrink_weight, shrink_bias, time_weight, time_bias, text_weight, text_bias, project_weight, query_bias, value_bias, output_weight, output_bias = weights
    padded = jnp.pad(latent, ((1, 1), (1, 1), (0, 0)))
    conv_out = depth_bias
    for offset_down in range(3):
        for offset_side in range(3):
            conv_out = conv_out + padded[offset_down:offset_down + H, offset_side:offset_side + W] * kernel[offset_down, offset_side]
    conv_out = low_back(conv_out)
    normed_one = low(layer_norm(conv_out))
    pre_act = low_back(jnp.einsum('hwc,cf->hwf', normed_one, expand_weight, precision=highest_mode) + expand_bias)
    activation = jax.nn.gelu(pre_act, approximate=False)
    col_norm = jnp.sqrt(lax.optimization_barrier(jnp.sum(activation * activation, axis=(0, 1))))
    denominator = jnp.mean(col_norm) + 1e-06
    mixed = low(response_gain * (activation * (col_norm / denominator)) + response_bias + activation)
    branch = low_back(jnp.einsum('hwf,fc->hwc', mixed, shrink_weight, precision=highest_mode))
    first_sum = latent + branch + shrink_bias
    modulation = jnp.dot(embedding, time_weight, precision=highest_mode) + time_bias
    second_sum = first_sum * (1.0 + modulation[:C]) + modulation[C:]
    normed_two = low(layer_norm(second_sum))
    keep_text = (1 - drop_item).astype(jnp.float32)
    text_in = low(jax.nn.silu(caption_item * keep_text))
    text_keys = low_back(low(jnp.dot(text_in, text_weight, precision=highest_mode) + text_bias))
    image_rows = normed_two.reshape(H * W, C)
    keys_in = jnp.concatenate([image_rows, text_keys], axis=0)
    query = low_back(low(jnp.dot(image_rows, project_weight[:, 0], precision=highest_mode) + query_bias))
    key_rows = low_back(low(jnp.dot(keys_in, project_weight[:, 1], precision=highest_mode)))
    value_rows = low_back(low(jnp.dot(keys_in, project_weight[:, 2], precision=highest_mode) + value_bias))
    query = query.reshape(H * W, HEADS, HEAD)
    key_rows = key_rows.reshape(H * W + TEXT, HEADS, HEAD)
    value_rows = value_rows.reshape(H * W + TEXT, HEADS, HEAD)
    scores = low_back(jnp.einsum('qhd,khd->hqk', query, key_rows, precision=highest_mode) * (1.0 / math.sqrt(HEAD)))
    valid_keys = jnp.arange(H * W + TEXT) < H * W + length_item
    scores = jnp.where(valid_keys[None, None, :], scores, -1e+30)
    probs = jax.nn.softmax(scores, axis=-1)
    attended = jnp.einsum('hqk,khd->qhd', low(probs), value_rows, precision=highest_mode).reshape(H * W, C)
    attended = low_back(low(attended))
    attention = low_back(jnp.dot(attended, output_weight, precision=highest_mode))
    return second_sum + attention.reshape(H, W, C) + output_bias

def reference(latents, depth_kernel, depth_bias, expand_weight, expand_bias, response_gain, response_bias, shrink_weight, shrink_bias, time_embed, time_weight, time_bias, caption, drop_flags, caption_lengths, text_weight, text_bias, project_weight, query_bias, value_bias, output_weight, output_bias, cotangent):
    weights = tuple((weight_item.astype(jnp.float32) for weight_item in (depth_kernel, depth_bias, expand_weight, expand_bias, response_gain, response_bias, shrink_weight, shrink_bias, time_weight, time_bias, text_weight, text_bias, project_weight, query_bias, value_bias, output_weight, output_bias)))
    embeds = time_embed.astype(jnp.float32)
    captions = caption.astype(jnp.float32)
    checked = jax.checkpoint(item_forward)

    def forward(weight_set, latent_all):
        return lax.map(lambda packed: checked(weight_set, *packed), (latent_all, embeds, captions, drop_flags, caption_lengths))
    result, pullback = jax.vjp(forward, weights, latents.astype(jnp.float32))
    weight_grads, latents_grad = pullback(cotangent.astype(jnp.float32))
    return (result.astype(jnp.bfloat16), latents_grad.astype(jnp.bfloat16), weight_grads[0], weight_grads[1], weight_grads[2], weight_grads[3], weight_grads[4], weight_grads[5], weight_grads[6], weight_grads[7], weight_grads[8], weight_grads[9], weight_grads[10], weight_grads[11], weight_grads[12], weight_grads[13], weight_grads[14], weight_grads[15], weight_grads[16])
```

```python
import math

import jax
import jax.numpy as jnp
from jax import lax
from jax.sharding import PartitionSpec as P

HEAD = 64
F32 = jnp.float32
BF16 = jnp.bfloat16
STREAMS = 1


def swap(values, axis, mask):
    size = lax.axis_size(axis)
    return lax.ppermute(values, axis, [(i, i ^ mask) for i in range(size)])


def halo_rows(shard, axis):
    size, length = (lax.axis_size(axis), shard.shape[1])
    up = [(i, i + 1) for i in range(size - 1)]
    down = [(j, i) for i, j in up]
    before = lax.ppermute(shard[:, length - 1 :], axis, up)
    after = lax.ppermute(shard[:, :1], axis, down)
    return before, after


def gather_rows(own):
    core = swap(own, "mp", 1)
    across = swap(own, "mp", 2)
    diagonal = swap(across, "mp", 1)
    return jnp.concatenate([own, across, core, diagonal], axis=1)


def scatter_rows(part):
    half = part.shape[1] // 2
    quarter = half // 2
    got = swap(part[:, half:], "mp", 1).astype(F32)
    kept = part[:, :half].astype(F32) + got
    across = swap(kept[:, quarter:].astype(BF16), "mp", 2).astype(F32)
    return kept[:, :quarter] + across


def sum_mp(values):
    values = values + swap(values, "mp", 1)
    return values + swap(values, "mp", 2)


def halve(grad, axis, bits, link=BF16):
    count = int(math.log2(lax.axis_size(axis)))
    grad = grad.reshape((2,) * count + grad.shape[1:])
    index = lax.axis_index(axis)
    left = list(range(count - 1, -1, -1))
    for bit in bits:
        place = left.index(bit)
        left.remove(bit)
        mine = (index >> bit) & 1
        sent = lax.dynamic_index_in_dim(grad, 1 - mine, place, keepdims=False)
        kept = lax.dynamic_index_in_dim(grad, mine, place, keepdims=False)
        got = swap(sent.astype(link), axis, 1 << bit)
        grad = kept.astype(F32) + got.astype(F32)
    return grad


def layer_norm(values):
    centred = values - jnp.mean(values, axis=-1, keepdims=True)
    inverse = lax.rsqrt(jnp.mean(centred * centred, axis=-1, keepdims=True) + 1e-06)
    return (centred * inverse, inverse)


def norm_back(normed, inverse, upstream):
    return inverse * (
        upstream
        - jnp.mean(upstream, axis=-1, keepdims=True)
        - normed * jnp.mean(upstream * normed, axis=-1, keepdims=True)
    )


def gelu_slope(values):
    cumulative = 0.5 * (1.0 + lax.erf(values * (1.0 / math.sqrt(2.0))))
    density = jnp.exp(-0.5 * values * values) * (1.0 / math.sqrt(2.0 * math.pi))
    return cumulative + values * density


def dot(spec, left, right):
    return jnp.einsum(spec, left, right, preferred_element_type=F32)


def attention(query, key, value, grad_out, lengths, positions):
    item_count, _, width = query.shape
    keys_total = key.shape[1]
    heads = width // HEAD
    score_scale = 1.0 / math.sqrt(HEAD)
    query = query.reshape(item_count, positions, heads, HEAD)
    key = key.reshape(item_count, keys_total, heads, HEAD)
    value = value.reshape(item_count, keys_total, heads, HEAD)
    grad_out = grad_out.reshape(item_count, positions, heads, HEAD)
    valid = jnp.arange(keys_total)[None, :] < (positions + lengths)[:, None]
    scores = dot("iqhd,ikhd->ihqk", query, key) * score_scale
    scores = jnp.where(valid[:, None, None, :], scores, -1e30)
    peak = jnp.max(scores, axis=-1, keepdims=True)
    exponent = jnp.exp(scores - peak)
    probs = exponent / jnp.sum(exponent, axis=-1, keepdims=True)
    probs_low = probs.astype(BF16)
    attended = dot("ihqk,ikhd->iqhd", probs_low, value)
    attended = attended.reshape(item_count, positions, width).astype(BF16)
    grad_probs = dot("iqhd,ikhd->ihqk", grad_out, value)
    grad_value = dot("ihqk,iqhd->ikhd", probs_low, grad_out)
    grad_scores = probs * (grad_probs - jnp.sum(grad_probs * probs, axis=-1, keepdims=True))
    grad_scores = grad_scores.astype(BF16)
    grad_query = dot("ihqk,ikhd->iqhd", grad_scores, key) * score_scale
    grad_key = dot("ihqk,iqhd->ikhd", grad_scores, query) * score_scale
    return (
        attended,
        grad_query.astype(BF16).reshape(item_count, positions, width),
        grad_key.astype(BF16).reshape(item_count, keys_total, width),
        grad_value.astype(BF16).reshape(item_count, keys_total, width),
    )


def shards(
    latents,
    depth_kernel,
    depth_bias,
    expand_weight,
    expand_bias,
    response_gain,
    response_bias,
    shrink_weight,
    shrink_bias,
    time_embed,
    time_weight,
    time_bias,
    caption,
    drop_flags,
    caption_lengths,
    text_weight,
    text_bias,
    project_weight,
    query_bias,
    value_bias,
    output_weight,
    output_bias,
    cotangent,
):
    items, slab, grid_width, channels = latents.shape
    dp_size, mp_size = lax.axis_size("dp"), lax.axis_size("mp")
    dp_bits = list(range(int(math.log2(dp_size))))
    rows = slab * grid_width
    positions = rows * mp_size
    hidden = expand_weight.shape[1]
    hidden_all = hidden * mp_size
    width = project_weight.shape[2]
    streams = STREAMS
    each = items // streams

    def cut(values, s):
        return values[s * each : (s + 1) * each]

    def flat(values):
        return values.reshape(values.shape[0] * values.shape[1], values.shape[2])

    kernel = depth_kernel.astype(F32)
    before, after = halo_rows(latents, "mp")
    grad_rows = [gather_rows(cut(cotangent, s).reshape(each, rows, channels)) for s in range(streams)]

    modulation = jnp.dot(
        time_embed, time_weight.astype(F32), precision=lax.Precision.HIGHEST
    ) + time_bias.astype(F32)
    keep_text = (1 - drop_flags).astype(F32)
    text_in = jax.nn.silu(caption.astype(F32) * keep_text[:, None, None]).astype(BF16)
    text_own = (dot("itk,kc->itc", text_in, text_weight) + text_bias.astype(F32)).astype(BF16)
    mp_index = lax.axis_index("mp")
    text_core = swap(text_own, "mp", 1)
    text_across = swap(text_own, "mp", 2)
    text_diag = swap(text_across, "mp", 1)
    pieces = (text_own, text_core, text_across, text_diag)

    def piece_of(holder):
        relation = mp_index ^ holder
        return lax.select_n(relation, *pieces)

    text_full = jnp.concatenate([piece_of(j) for j in range(mp_size)], axis=2)

    halo_in = jnp.concatenate([before, latents, after], axis=1)
    padded_in = jnp.pad(halo_in, ((0, 0), (0, 0), (1, 1), (0, 0)))

    state = []
    for s in range(streams):
        window = cut(padded_in, s)
        conv_out = depth_bias.astype(F32)
        for down in range(3):
            for side in range(3):
                conv_out = (
                    conv_out
                    + window[:, down : down + slab, side : side + grid_width].astype(F32)
                    * kernel[down, side]
                )
        normed_one, inverse_one = layer_norm(conv_out.reshape(each, rows, channels))
        gathered_one = gather_rows(normed_one.astype(BF16))
        state.append(dict(normed_one=normed_one, inverse_one=inverse_one, gathered_one=gathered_one))

    gain = response_gain.astype(F32)
    for s in range(streams):
        st = state[s]
        pre = dot("irc,cf->irf", st["gathered_one"], expand_weight) + expand_bias.astype(F32)
        act = jax.nn.gelu(pre, approximate=False)
        col_norm = jnp.sqrt(jnp.sum(act * act, axis=1))
        norm_total = sum_mp(jnp.sum(col_norm, axis=1))
        denominator = norm_total / hidden_all + 1e-06
        ratio = (col_norm / denominator[:, None])[:, None, :]
        mixed = (gain * (act * ratio) + response_bias.astype(F32) + act).astype(BF16)
        shrink_part = dot("irf,fc->irc", mixed, shrink_weight).astype(BF16)
        branch = scatter_rows(shrink_part)
        own = cut(latents, s).reshape(each, rows, channels).astype(F32)
        first_sum = own + branch + shrink_bias.astype(F32)
        mod = cut(modulation, s)
        scale = mod[:, None, :channels]
        shift = mod[:, None, channels:]
        second_sum = first_sum * (1.0 + scale) + shift
        normed_two, inverse_two = layer_norm(second_sum)
        gathered_two = gather_rows(normed_two.astype(BF16))
        st.update(
            pre=pre, act=act, col_norm=col_norm, denominator=denominator, ratio=ratio, mixed=mixed,
            first_sum=first_sum, scale=scale, second_sum=second_sum, normed_two=normed_two,
            inverse_two=inverse_two, gathered_two=gathered_two,
        )

    for s in range(streams):
        st = state[s]
        image = st["gathered_two"]
        keys_in = jnp.concatenate([image, cut(text_full, s)], axis=1)
        query = (dot("isc,cd->isd", image, project_weight[:, 0]) + query_bias.astype(F32)).astype(BF16)
        key = dot("isc,cd->isd", keys_in, project_weight[:, 1]).astype(BF16)
        value = (dot("isc,cd->isd", keys_in, project_weight[:, 2]) + value_bias.astype(F32)).astype(BF16)
        grad_att = dot("isc,dc->isd", grad_rows[s], output_weight).astype(BF16)
        attended, grad_query, grad_key, grad_value = attention(
            query, key, value, grad_att, cut(caption_lengths, s), positions
        )
        grad_keys = dot("isd,cd->isc", grad_key, project_weight[:, 1]) + dot(
            "isd,cd->isc", grad_value, project_weight[:, 2]
        )
        grad_image = (
            dot("isd,cd->isc", grad_query, project_weight[:, 0]) + grad_keys[:, :positions]
        ).astype(BF16)
        grad_norm_two = scatter_rows(grad_image)
        st.update(
            keys_in=keys_in, attended=attended, grad_query=grad_query, grad_key=grad_key,
            grad_value=grad_value, grad_norm_two=grad_norm_two,
            grad_text_part=grad_keys[:, positions:].astype(BF16),
        )

    grad_text_part = jnp.concatenate([st["grad_text_part"] for st in state], axis=0)
    columns = grad_text_part.reshape(items, -1, mp_size, width)

    def columns_of(holder):
        return lax.dynamic_index_in_dim(columns, holder, 2, keepdims=False)

    sent = jnp.stack([columns_of(mp_index ^ 1), columns_of(mp_index ^ 3)])
    kept = jnp.stack([columns_of(mp_index), columns_of(mp_index ^ 2)])
    kept = kept.astype(F32) + swap(sent, "mp", 1).astype(F32)
    grad_text = (kept[0] + swap(kept[1].astype(BF16), "mp", 2).astype(F32)).astype(BF16)
    grad_text_weight = dot("itk,itc->kc", text_in, grad_text)
    grad_text_bias = jnp.sum(grad_text.astype(F32), axis=(0, 1))

    results = []
    for s in range(streams):
        st = state[s]
        grad_top = cut(cotangent, s).reshape(each, rows, channels).astype(F32)
        grad_second = grad_top + norm_back(st["normed_two"], st["inverse_two"], st["grad_norm_two"])
        grad_first = grad_second * (1.0 + st["scale"])
        first_rows = gather_rows(grad_first.astype(BF16))
        st.update(
            grad_first=grad_first, first_rows=first_rows,
            grad_modul=jnp.concatenate(
                [jnp.sum(grad_second * st["first_sum"], axis=1), jnp.sum(grad_second, axis=1)], axis=1
            ),
            grad_out_bias=jnp.sum(grad_top, axis=(0, 1)),
            grad_shrink_bias=jnp.sum(grad_first, axis=(0, 1)),
        )
        out_part = dot("isd,dc->isc", st["attended"], output_weight).astype(BF16)
        attention_out = scatter_rows(out_part)
        results.append(
            (st["second_sum"] + attention_out + output_bias.astype(F32)).astype(BF16)
        )

    def both(name):
        return flat(jnp.concatenate([st[name] for st in state], axis=0))

    image_all = both("gathered_two")
    keys_all = both("keys_in")
    grad_query_all, grad_key_all, grad_value_all = both("grad_query"), both("grad_key"), both("grad_value")
    attended_all = both("attended")
    grad_rows_all = flat(jnp.concatenate(grad_rows, axis=0))
    chunk = channels // dp_size
    attention_grads = jnp.concatenate(
        [
            dot("rc,rd->cd", image_all, grad_query_all).astype(BF16),
            dot("rc,rd->cd", keys_all, grad_key_all).astype(BF16),
            dot("rc,rd->cd", keys_all, grad_value_all).astype(BF16),
            dot("rc,rd->cd", grad_rows_all, attended_all).astype(BF16),
        ],
        axis=1,
    ).reshape(dp_size, chunk, 4 * width)
    clip = text_weight.shape[0]
    text_grads = grad_text_weight.astype(BF16).reshape(dp_size, clip // dp_size, width)
    attention_sent = halve(attention_grads, "dp", dp_bits)
    text_sent = halve(text_grads, "dp", dp_bits)

    for s in range(streams):
        st = state[s]
        grad_mixed = dot("irc,fc->irf", st["first_rows"], shrink_weight)
        st["grad_gain"] = jnp.sum(grad_mixed * st["act"] * st["ratio"], axis=(0, 1))
        st["grad_response_bias"] = jnp.sum(grad_mixed, axis=(0, 1))
        grad_ratio = jnp.sum(grad_mixed * gain * st["act"], axis=1)
        cross = sum_mp(jnp.sum(grad_ratio * st["col_norm"], axis=1))
        denominator = st["denominator"]
        grad_col = (
            grad_ratio / denominator[:, None]
            - (cross / (hidden_all * denominator * denominator))[:, None]
        )
        grad_act = (
            grad_mixed * (gain * st["ratio"] + 1.0)
            + (grad_col / st["col_norm"])[:, None, :] * st["act"]
        )
        st["grad_pre"] = (grad_act * gelu_slope(st["pre"])).astype(BF16)

    grad_pre_all = both("grad_pre")
    shrink_grads = dot("rc,rf->cf", both("first_rows"), both("mixed")).astype(BF16)
    shrink_sent = halve(shrink_grads.reshape(dp_size, chunk, hidden), "dp", dp_bits)
    expand_grads = dot("rc,rf->cf", both("gathered_one"), grad_pre_all).astype(BF16)
    expand_sent = halve(
        expand_grads.reshape(dp_size, chunk, hidden), "dp", dp_bits[1:] + dp_bits[:1]
    )

    latents_grads = []
    conv_grads = []
    grad_conv_all = []
    for s in range(streams):
        st = state[s]
        grad_norm_part = dot("irf,cf->irc", st["grad_pre"], expand_weight).astype(BF16)
        grad_norm_one = scatter_rows(grad_norm_part)
        grad_conv = norm_back(st["normed_one"], st["inverse_one"], grad_norm_one).astype(BF16)
        grad_conv_all.append(grad_conv.reshape(each, slab, grid_width, channels))
    grad_conv = jnp.concatenate(grad_conv_all, axis=0)
    back_before, back_after = halo_rows(grad_conv, "mp")
    halo_grad = jnp.concatenate([back_before, grad_conv, back_after], axis=1)
    padded_grad = jnp.pad(halo_grad, ((0, 0), (0, 0), (1, 1), (0, 0)))
    grad_conv_full = grad_conv.astype(F32)
    grad_first = jnp.concatenate([st["grad_first"] for st in state], axis=0).reshape(latents.shape)
    conv_back = jnp.zeros_like(grad_first)
    kernel_rows = []
    for down in range(3):
        for side in range(3):
            window_in = padded_in[:, down : down + slab, side : side + grid_width].astype(F32)
            kernel_rows.append(jnp.sum(window_in * grad_conv_full, axis=(0, 1, 2)))
            window_grad = padded_grad[
                :, 2 - down : 2 - down + slab, 2 - side : 2 - side + grid_width
            ].astype(F32)
            conv_back = conv_back + window_grad * kernel[down, side]
    kernel_rows.append(jnp.sum(grad_conv_full, axis=(0, 1, 2)))
    latents_grad = (grad_first + conv_back).astype(BF16)
    tail = jnp.stack(kernel_rows)
    taps = tail.shape[0]
    tail = jnp.transpose(tail.reshape(taps, dp_size, chunk), (1, 0, 2))
    tail = halve(tail, "dp", dp_bits, F32)
    tail = jnp.transpose(tail.reshape(taps, mp_size, chunk // mp_size), (1, 0, 2))
    tail = halve(tail, "mp", [0, 1], F32)

    grad_modul = jnp.concatenate([st["grad_modul"] for st in state], axis=0)
    shared = sum_mp(
        jnp.concatenate(
            [
                grad_modul,
                jnp.concatenate(
                    [
                        sum(st["grad_out_bias"] for st in state),
                        sum(st["grad_shrink_bias"] for st in state),
                    ]
                )[None],
            ],
            axis=0,
        )
    )
    grad_modul = shared[:items]
    grad_out_bias, grad_shrink_bias = shared[items, :channels], shared[items, channels:]
    grad_time_bias = jnp.sum(grad_modul, axis=0)
    time_rows = grad_modul
    embeds = time_embed
    dp_index = lax.axis_index("dp")
    for bit in reversed(dp_bits):
        half = time_rows.shape[1] // 2
        mine = (dp_index >> bit) & 1
        sent = lax.dynamic_slice_in_dim(time_rows, (1 - mine) * half, half, axis=1)
        kept = lax.dynamic_slice_in_dim(time_rows, mine * half, half, axis=1)
        got = swap(jnp.concatenate([sent, embeds], axis=1), "dp", 1 << bit)
        time_rows = jnp.concatenate([kept, got[:, :half]], axis=0)
        embeds = jnp.concatenate([embeds, got[:, half:]], axis=0)
    time_weight_grad = jnp.dot(embeds.T, time_rows, precision=lax.Precision.HIGHEST)

    vectors = [
        jnp.sum(grad_query_all.astype(F32), axis=0),
        jnp.sum(grad_value_all.astype(F32), axis=0),
        grad_text_bias,
        jnp.sum(grad_pre_all.astype(F32), axis=0),
        sum(st["grad_gain"] for st in state),
        sum(st["grad_response_bias"] for st in state),
        grad_shrink_bias,
        grad_time_bias,
        grad_out_bias,
    ]
    packed = jnp.concatenate([v.reshape(dp_size, -1) for v in vectors], axis=1)
    packed = halve(packed, "dp", dp_bits, F32)
    small, at = ([], 0)
    for v in vectors:
        length = v.shape[0] // dp_size
        small.append(packed[at : at + length])
        at += length

    grid = (items, slab, grid_width, channels)
    return (
        jnp.concatenate(results, axis=0).reshape(grid),
        latents_grad,
        tail[: taps - 1].reshape(3, 3, chunk // mp_size),
        tail[taps - 1],
        expand_sent,
        small[3],
        small[4],
        small[5],
        shrink_sent.T,
        small[6],
        time_weight_grad,
        small[7],
        text_sent,
        small[2],
        attention_sent[:, : 3 * width].reshape(chunk, 3, width),
        small[0],
        small[1],
        attention_sent[:, 3 * width :].T,
        small[8],
    )


def solution(mesh):
    return jax.shard_map(
        shards,
        mesh=mesh,
        in_specs=(
            P("dp", "mp", None, None),
            P(),
            P(),
            P(None, "mp"),
            P("mp"),
            P("mp"),
            P("mp"),
            P("mp", None),
            P(),
            P("dp", None),
            P(),
            P(),
            P("dp", None, None),
            P("dp"),
            P("dp"),
            P(None, "mp"),
            P("mp"),
            P(None, None, "mp"),
            P("mp"),
            P("mp"),
            P("mp", None),
            P(),
            P("dp", "mp", None, None),
        ),
        out_specs=(
            P("dp", "mp", None, None),
            P("dp", "mp", None, None),
            P(None, None, ("dp", "mp")),
            P(("dp", "mp")),
            P("dp", "mp"),
            P(("mp", "dp")),
            P(("mp", "dp")),
            P(("mp", "dp")),
            P("mp", "dp"),
            P("dp"),
            P(None, "dp"),
            P("dp"),
            P("dp", "mp"),
            P(("mp", "dp")),
            P("dp", None, "mp"),
            P(("mp", "dp")),
            P(("mp", "dp")),
            P("mp", "dp"),
            P("dp"),
        ),
        check_vma=False,
    )
```

```python
import functools
import math

import jax
import jax.numpy as jnp
from jax import lax
from jax.experimental import pallas as pl
from jax.experimental.pallas import tpu as pltpu
from jax.sharding import PartitionSpec as P

HEAD = 64
LANES = 128
F32 = jnp.float32
BF16 = jnp.bfloat16
STREAMS = 1


def swap(values, axis, mask):
    size = lax.axis_size(axis)
    return lax.ppermute(values, axis, [(i, i ^ mask) for i in range(size)])


def after(values, other):
    return lax.optimization_barrier((values, other))[0]


def halo_rows(shard, axis):
    size, length = (lax.axis_size(axis), shard.shape[1])
    up = [(i, i + 1) for i in range(size - 1)]
    down = [(j, i) for i, j in up]
    before = lax.ppermute(shard[:, length - 1 :], axis, up)
    after_rows = lax.ppermute(shard[:, :1], axis, down)
    return before, after_rows


def gather_rows(own, *extra):
    across = swap(own, "mp", 2)
    core = swap(own, "mp", 1)
    diagonal = swap(across, "mp", 1)
    return jnp.concatenate([own, across, core, diagonal, *extra], axis=1)


def scatter_rows(part, rows):
    got = swap(part[:, 2 * rows : 4 * rows], "mp", 1).astype(F32)
    kept = part[:, : 2 * rows].astype(F32) + got
    across = swap(kept[:, rows:].astype(BF16), "mp", 2).astype(F32)
    return kept[:, :rows] + across


def sum_mp(values):
    values = values + swap(values, "mp", 1)
    return values + swap(values, "mp", 2)


def halve(grads, axis, bits, link=BF16, hold=None):
    count = int(math.log2(lax.axis_size(axis)))
    grads = [grad.reshape((2,) * count + grad.shape[1:]) for grad in grads]
    index = lax.axis_index(axis)
    left = list(range(count - 1, -1, -1))
    total = None
    for turn, bit in enumerate(bits):
        place = left.index(bit)
        left.remove(bit)
        mine = (index >> bit) & 1
        pick = lambda grad, side: lax.dynamic_index_in_dim(grad, side, place, keepdims=False)
        sent = jnp.concatenate([pick(grad, 1 - mine).astype(link) for grad in grads], axis=-1)
        got = swap(sent, axis, 1 << bit)
        if hold is not None and turn < len(hold) and hold[turn] is not None:
            got = after(got, hold[turn])
        kept = jnp.concatenate([pick(grad, mine) for grad in grads], axis=-1)
        total = kept.astype(F32) + got.astype(F32)
        grads = [total]
    return total


def layer_norm(values):
    centred = values - jnp.mean(values, axis=-1, keepdims=True)
    inverse = lax.rsqrt(jnp.mean(centred * centred, axis=-1, keepdims=True) + 1e-06)
    return (centred * inverse, inverse)


def norm_back(normed, inverse, upstream):
    return inverse * (
        upstream
        - jnp.mean(upstream, axis=-1, keepdims=True)
        - normed * jnp.mean(upstream * normed, axis=-1, keepdims=True)
    )


def dot(spec, left, right):
    return jnp.einsum(spec, left, right, preferred_element_type=F32)


def attend_kernel(positions, lengths, q_ref, k_ref, v_ref, g_ref, o_ref, d_ref):
    item = pl.program_id(0)
    pair = pl.program_id(1)
    pairs = pl.num_programs(1)
    lanes = q_ref.shape[1]
    keys = k_ref.shape[0]
    limit = positions + lengths[item]
    lane = lax.broadcasted_iota(jnp.int32, (1, lanes), 1)
    scale = 1.0 / math.sqrt(HEAD)
    query = (q_ref[:positions].astype(F32) * scale).astype(BF16)
    key, value, grad = k_ref[...], v_ref[...], g_ref[...]
    tail = lax.broadcasted_iota(jnp.int32, (1, keys - positions), 1) + positions
    bias = jnp.concatenate([jnp.zeros((1, positions), F32), jnp.where(tail < limit, 0.0, -1e30)], axis=1)
    outs, d_queries, d_keys, d_values = [], [], [], []
    nt = (((1,), (1,)), ((), ()))
    tn = (((0,), (0,)), ((), ()))
    for head in range(lanes // HEAD):
        here = (lane >= head * HEAD) & (lane < (head + 1) * HEAD)
        first = HEAD if head == 0 else 0
        query_head = jnp.where(here, query, jnp.zeros_like(query))
        value_ones = jnp.where(here, value, jnp.ones_like(value))
        scores = lax.dot_general(query_head, key, nt, preferred_element_type=F32) + bias
        peak = jnp.max(scores, axis=1, keepdims=True)
        weight = jnp.exp(scores - peak)
        weight_low = weight.astype(BF16)
        total = lax.dot_general(weight_low, value_ones, (((1,), (0,)), ((), ())), preferred_element_type=F32)
        inverse = 1.0 / total[:, first : first + 1]
        out = total * inverse
        outs.append(out)
        grad_head = jnp.where(here, grad, jnp.zeros_like(grad))
        dot = jnp.sum(grad_head.astype(F32) * out, axis=1, keepdims=True)
        dot_high = dot.astype(BF16)
        dot_low = (dot - dot_high.astype(F32)).astype(BF16)
        grad_ext = jnp.where(lane == first, -dot_high, jnp.where(lane == first + 1, -dot_low, grad_head))
        spread = lax.dot_general(grad_ext, value_ones, nt, preferred_element_type=F32)
        d_scores = (weight * spread).astype(BF16)
        d_query = lax.dot_general(d_scores, key, (((1,), (0,)), ((), ())), preferred_element_type=F32)
        d_queries.append(d_query * (inverse * scale))
        query_scaled = (query.astype(F32) * inverse).astype(BF16)
        grad_scaled = (grad.astype(F32) * inverse).astype(BF16)
        rows = slice(head * HEAD, (head + 1) * HEAD)
        d_keys.append(lax.dot_general(query_scaled.T[rows], d_scores, (((1,), (0,)), ((), ())), preferred_element_type=F32))
        d_values.append(lax.dot_general(grad_scaled.T[rows], weight_low, (((1,), (0,)), ((), ())), preferred_element_type=F32))
    low_half = lane < HEAD
    o_ref[...] = jnp.where(low_half, outs[0], outs[1]).astype(BF16)
    d_query = jnp.where(low_half, d_queries[0], d_queries[1]).astype(BF16)
    at = pl.multiple_of(pair * lanes, lanes)
    step = pairs * lanes
    d_ref[:positions, pl.ds(at, lanes)] = d_query
    d_ref[positions:, pl.ds(at, lanes)] = jnp.zeros((keys - positions, lanes), BF16)
    d_ref[:, pl.ds(at + step, lanes)] = jnp.concatenate(d_keys, axis=0).T.astype(BF16)
    d_ref[:, pl.ds(at + 2 * step, lanes)] = jnp.concatenate(d_values, axis=0).T.astype(BF16)

def attend(qkv, grad, lengths, positions):
    n, keys, w3 = qkv.shape
    w = w3 // 3
    pairs = w // 128
    spec = lambda off: pl.BlockSpec((None, keys, 128), lambda i, p, l: (i, 0, off * pairs + p))
    own = pl.BlockSpec((None, positions, 128), lambda i, p, l: (i, 0, p))
    return pl.pallas_call(
        functools.partial(attend_kernel, positions),
        out_shape=(jax.ShapeDtypeStruct((n, positions, w), BF16), jax.ShapeDtypeStruct((n, keys, w3), BF16)),
        grid_spec=pltpu.PrefetchScalarGridSpec(
            num_scalar_prefetch=1, grid=(n, pairs),
            in_specs=[spec(0), spec(1), spec(2), own],
            out_specs=[own, pl.BlockSpec((None, keys, w3), lambda i, p, l: (i, 0, 0))],
        ),
        compiler_params=pltpu.CompilerParams(vmem_limit_bytes=48 << 20),
        cost_estimate=pl.CostEstimate(flops=n * pairs * 2 * 12 * positions * keys * 128, bytes_accessed=n * keys * w * 14, transcendentals=n * pairs * 2 * positions * keys),
    )(lengths, qkv, qkv, qkv, grad)

def erf(x):
    x = jnp.clip(x, -3.832506856900711, 3.832506856900711)
    y = x * x
    a = [0.00022905065861350646, 0.0034082910107109506, 0.050955695062380861, 0.18520832239976145, 1.128379143519084]
    b = [-1.1791602954361697e-7, 0.000023547966471313185, 0.0010179625278914885, 0.014070470171167667, 0.11098505178285362, 0.49746925110067538, 1.0]
    p = a[0]
    for c in a[1:]: p = p * y + c
    q = b[0]
    for c in b[1:]: q = q * y + c
    return x * p / q

def expand_kernel(item_rows, x_ref, w_ref, b_ref, act_ref, slope_ref, sq_ref):
    items = x_ref.shape[0] // item_rows
    bias = b_ref[...].astype(F32)
    for i in range(items):
        rows = slice(i * item_rows, (i + 1) * item_rows)
        pre = jnp.dot(x_ref[rows], w_ref[...], preferred_element_type=F32) + bias
        cumulative = 0.5 * (1.0 + erf(pre * (1.0 / math.sqrt(2.0))))
        density = jnp.exp(-0.5 * pre * pre) * (1.0 / math.sqrt(2.0 * math.pi))
        act = pre * cumulative
        act_ref[rows] = act.astype(BF16)
        slope_ref[rows] = (cumulative + pre * density).astype(BF16)
        sq_ref[i] = jnp.sum(act * act, axis=0, keepdims=True)

def expand(x, w, b, item_rows, tile=256):
    rows, c = x.shape
    f = w.shape[1]
    items = rows // item_rows
    out = pl.BlockSpec((rows, tile), lambda j: (0, j))
    return pl.pallas_call(
        functools.partial(expand_kernel, item_rows),
        out_shape=(jax.ShapeDtypeStruct((rows, f), BF16), jax.ShapeDtypeStruct((rows, f), BF16), jax.ShapeDtypeStruct((items, 1, f), F32)),
        grid=(f // tile,),
        in_specs=[pl.BlockSpec((rows, c), lambda j: (0, 0)), pl.BlockSpec((c, tile), lambda j: (0, j)), pl.BlockSpec((1, tile), lambda j: (0, j))],
        out_specs=(out, out, pl.BlockSpec((items, 1, tile), lambda j: (0, 0, j))),
        compiler_params=pltpu.CompilerParams(vmem_limit_bytes=48 << 20),
        cost_estimate=pl.CostEstimate(flops=2 * rows * c * f, bytes_accessed=2 * (rows * c + c * f + 2 * rows * f), transcendentals=rows * f),
    )(x, w, b.reshape(1, f))


def shards(
    latents,
    depth_kernel,
    depth_bias,
    expand_weight,
    expand_bias,
    response_gain,
    response_bias,
    shrink_weight,
    shrink_bias,
    time_embed,
    time_weight,
    time_bias,
    caption,
    drop_flags,
    caption_lengths,
    text_weight,
    text_bias,
    project_weight,
    query_bias,
    value_bias,
    output_weight,
    output_bias,
    cotangent,
):
    items, slab, grid_width, channels = latents.shape
    dp_size, mp_size = lax.axis_size("dp"), lax.axis_size("mp")
    dp_bits = list(range(int(math.log2(dp_size))))
    dp_turned = dp_bits[1:] + dp_bits[:1]
    dp_index, mp_index = lax.axis_index("dp"), lax.axis_index("mp")
    rows = slab * grid_width
    positions = rows * mp_size
    hidden = expand_weight.shape[1]
    hidden_all = hidden * mp_size
    width = project_weight.shape[2]
    text_slots = caption.shape[1]
    text_rows = -(-text_slots // LANES) * LANES
    keys = positions + text_rows
    chunk = channels // dp_size
    streams = STREAMS
    each = items // streams

    def cut(values, s):
        return values[s * each : (s + 1) * each]

    def own_rows(values, s):
        return cut(values, s).reshape(each, rows, channels)

    kernel = depth_kernel.astype(F32)
    before, after_rows = halo_rows(latents, "mp")
    halo_in = jnp.concatenate([before, latents, after_rows], axis=1)
    padded_in = jnp.pad(halo_in, ((0, 0), (0, 0), (1, 1), (0, 0)))

    state = []
    for s in range(streams):
        window = cut(padded_in, s)
        conv_out = depth_bias.astype(F32)
        for down in range(3):
            for side in range(3):
                conv_out = (
                    conv_out
                    + window[:, down : down + slab, side : side + grid_width].astype(F32)
                    * kernel[down, side]
                )
        normed_one, inverse_one = layer_norm(conv_out.reshape(each, rows, channels))
        gathered_one = gather_rows(normed_one.astype(BF16)).reshape(each * positions, channels)
        state.append(dict(normed_one=normed_one, inverse_one=inverse_one, gathered_one=gathered_one))

    modulation = jnp.dot(
        time_embed, time_weight.astype(F32), precision=lax.Precision.HIGHEST
    ) + time_bias.astype(F32)
    keep_text = (1 - drop_flags).astype(F32)
    text_in = jax.nn.silu(caption.astype(F32) * keep_text[:, None, None]).astype(BF16)
    text_own = (dot("itk,kc->itc", text_in, text_weight) + text_bias.astype(F32)).astype(BF16)
    text_core = swap(text_own, "mp", 1)
    text_across = swap(text_own, "mp", 2)
    text_diag = swap(text_across, "mp", 1)
    pieces = (text_own, text_core, text_across, text_diag)
    text_full = jnp.concatenate(
        [lax.select_n(mp_index ^ holder, *pieces) for holder in range(mp_size)], axis=2
    )
    text_full = jnp.pad(text_full, ((0, 0), (0, text_rows - text_slots), (0, 0)))
    project = project_weight.reshape(channels, 3 * width)
    project_bias = jnp.concatenate([query_bias, jnp.zeros_like(query_bias), value_bias]).astype(F32)

    gain = response_gain.astype(F32)
    for s in range(streams):
        st = state[s]
        grad_rows = gather_rows(own_rows(cotangent, s))
        act, slope, squares = expand(st["gathered_one"], expand_weight, expand_bias, positions)
        act = act.reshape(each, positions, hidden)
        slope = slope.reshape(each, positions, hidden)
        col_norm = jnp.sqrt(squares[:, 0])
        norm_total = sum_mp(jnp.sum(col_norm, axis=1))
        denominator = norm_total / hidden_all + 1e-06
        ratio = (col_norm / denominator[:, None])[:, None, :]
        act_full = act.astype(F32)
        mixed = (gain * (act_full * ratio) + response_bias.astype(F32) + act_full).astype(BF16)
        shrink_part = dot("irf,fc->irc", mixed, shrink_weight).astype(BF16)
        branch = scatter_rows(shrink_part, rows)
        first_sum = own_rows(latents, s).astype(F32) + branch + shrink_bias.astype(F32)
        mod = cut(modulation, s)
        scale = mod[:, None, :channels]
        shift = mod[:, None, channels:]
        second_sum = first_sum * (1.0 + scale) + shift
        normed_two, inverse_two = layer_norm(second_sum)
        keys_in = gather_rows(normed_two.astype(BF16), cut(text_full, s))
        st.update(
            grad_rows=grad_rows, act=act, slope=slope, col_norm=col_norm, denominator=denominator,
            ratio=ratio, mixed=mixed, first_sum=first_sum, scale=scale, second_sum=second_sum,
            normed_two=normed_two, inverse_two=inverse_two, keys_in=keys_in,
        )

    for s in range(streams):
        st = state[s]
        qkv = (dot("isc,cd->isd", st["keys_in"], project) + project_bias).astype(BF16)
        grad_att = dot("isc,dc->isd", st["grad_rows"], output_weight).astype(BF16)
        attended, grad_qkv = attend(qkv, grad_att, cut(caption_lengths, s), positions)
        grad_keys = dot("isd,cd->isc", grad_qkv, project).astype(BF16)
        grad_norm_two = scatter_rows(grad_keys, rows)
        grad_top = own_rows(cotangent, s).astype(F32)
        grad_second = grad_top + norm_back(st["normed_two"], st["inverse_two"], grad_norm_two)
        grad_first = grad_second * (1.0 + st["scale"])
        first_rows = gather_rows(grad_first.astype(BF16))
        out_part = dot("isd,dc->isc", attended, output_weight).astype(BF16)
        attention_out = scatter_rows(out_part, rows)
        result = (st["second_sum"] + attention_out + output_bias.astype(F32)).astype(BF16)
        st.update(
            attended=attended, grad_qkv=grad_qkv, grad_keys=grad_keys, grad_first=grad_first,
            first_rows=first_rows, result=result,
            grad_modul=jnp.concatenate(
                [jnp.sum(grad_second * st["first_sum"], axis=1), jnp.sum(grad_second, axis=1)], axis=1
            ),
            grad_out_bias=jnp.sum(grad_top, axis=(0, 1)),
            grad_shrink_bias=jnp.sum(grad_first, axis=(0, 1)),
        )

    def both(name):
        joined = jnp.concatenate([st[name] for st in state], axis=0)
        return joined.reshape(-1, joined.shape[-1])

    columns = jnp.concatenate([st["grad_keys"][:, positions : positions + text_slots] for st in state], axis=0)
    columns = [columns[:, :, i * width : (i + 1) * width] for i in range(mp_size)]

    def columns_of(holder):
        return lax.select_n(holder, *columns)

    sent = jnp.stack([columns_of(mp_index ^ 1), columns_of(mp_index ^ 3)])
    kept = jnp.stack([columns_of(mp_index), columns_of(mp_index ^ 2)])
    kept = kept.astype(F32) + swap(sent, "mp", 1).astype(F32)
    grad_text = (kept[0] + swap(kept[1].astype(BF16), "mp", 2).astype(F32)).astype(BF16)
    clip = text_weight.shape[0]
    text_grads = dot("itk,itc->kc", text_in, grad_text).astype(BF16).reshape(dp_size, clip // dp_size, width)
    text_grads = jnp.pad(text_grads, ((0, 0), (0, chunk - clip // dp_size), (0, 0)))
    grad_text_bias = jnp.sum(grad_text.astype(F32), axis=(0, 1))

    grad_qkv_all = both("grad_qkv")
    project_grads = dot("rc,rd->cd", both("keys_in"), grad_qkv_all).astype(BF16)
    output_grads = dot("rc,rd->cd", both("grad_rows"), both("attended")).astype(BF16)
    grad_qkv_sum = jnp.sum(grad_qkv_all.astype(F32), axis=0)
    attention_sent = halve(
        [
            project_grads.reshape(dp_size, chunk, 3 * width),
            output_grads.reshape(dp_size, chunk, width),
            text_grads,
        ],
        "dp",
        dp_bits,
        hold=[state[-1]["first_rows"]],
    )

    for s in range(streams):
        st = state[s]
        grad_mixed = dot("irc,fc->irf", st["first_rows"], shrink_weight)
        act = st["act"].astype(F32)
        weighted = jnp.sum(grad_mixed * act, axis=1)
        st["grad_gain"] = jnp.sum(weighted * st["ratio"][:, 0], axis=0)
        st["grad_response_bias"] = jnp.sum(grad_mixed, axis=(0, 1))
        grad_ratio = gain * weighted
        cross = sum_mp(jnp.sum(grad_ratio * st["col_norm"], axis=1))
        denominator = st["denominator"]
        grad_col = (
            grad_ratio / denominator[:, None]
            - (cross / (hidden_all * denominator * denominator))[:, None]
        )
        grad_act = (
            grad_mixed.astype(BF16).astype(F32) * (gain * st["ratio"] + 1.0)
            + (grad_col / st["col_norm"])[:, None, :] * act
        )
        st["grad_pre"] = (grad_act * st["slope"].astype(F32)).astype(BF16)

    def send(grad, vectors):
        extra = jnp.concatenate([v.reshape(dp_size, -1) for v in vectors], axis=1)
        count = -(-extra.shape[1] // hidden)
        extra = jnp.pad(extra, ((0, 0), (0, count * hidden - extra.shape[1])))
        grad = jnp.concatenate(
            [grad.reshape(dp_size, chunk, hidden), extra.astype(BF16).reshape(dp_size, count, hidden)], axis=1
        )
        half = hidden // 2
        got = jnp.concatenate(
            [
                halve([grad[:, :, :half]], "dp", dp_bits),
                halve([grad[:, :, half:]], "dp", dp_turned),
            ],
            axis=1,
        )
        flat = got[chunk:].reshape(-1)
        small, at = ([], 0)
        for v in vectors:
            small.append(flat[at : at + v.size // dp_size])
            at += v.size // dp_size
        return got[:chunk], small

    all_items = items * dp_size
    grad_modul = jnp.concatenate([st["grad_modul"] for st in state], axis=0)
    columns_each = grad_modul.shape[1] // dp_size
    place = dp_index * items

    def placed(values):
        zeros = jnp.zeros(values.shape[:1] + (all_items,) + values.shape[2:], values.dtype)
        return lax.dynamic_update_slice_in_dim(zeros, values, place, axis=1)

    modul_slots = placed(
        jnp.transpose(grad_modul.reshape(items, dp_size, columns_each), (1, 0, 2))
    )
    embed_high = time_embed.astype(BF16).astype(F32)
    embed_slots = [
        placed(jnp.broadcast_to(v, (dp_size,) + v.shape)) for v in (embed_high, time_embed - embed_high)
    ]
    shrink_grads = dot("rc,rf->cf", both("first_rows"), both("mixed")).astype(BF16)
    shrink_sent, shrink_small = send(
        shrink_grads,
        [
            modul_slots,
            *embed_slots,
            sum(st["grad_out_bias"] for st in state),
            sum(st["grad_shrink_bias"] for st in state),
        ],
    )

    grad_pre_all = both("grad_pre")
    expand_grads = dot("rc,rf->cf", both("gathered_one"), grad_pre_all).astype(BF16)
    expand_sent, expand_small = send(
        expand_grads,
        [
            jnp.sum(grad_pre_all.astype(F32), axis=0),
            sum(st["grad_gain"] for st in state),
            sum(st["grad_response_bias"] for st in state),
            grad_qkv_sum[:width],
            grad_qkv_sum[2 * width :],
            grad_text_bias,
        ],
    )
    shared = sum_mp(jnp.concatenate([shrink_small[0], shrink_small[3], shrink_small[4]]))
    grad_modul = shared[: all_items * columns_each].reshape(all_items, columns_each)
    grad_out_bias, grad_shrink_bias = jnp.split(shared[all_items * columns_each :], 2)
    embeds = (shrink_small[1] + shrink_small[2]).reshape(all_items, -1)
    time_weight_grad = jnp.dot(embeds.T, grad_modul, precision=lax.Precision.HIGHEST)
    time_bias_grad = jnp.sum(grad_modul, axis=0)

    grad_conv_all = []
    for s in range(streams):
        st = state[s]
        grad_norm_part = dot("irf,cf->irc", st["grad_pre"], expand_weight).astype(BF16)
        grad_norm_one = scatter_rows(grad_norm_part, rows)
        grad_conv = norm_back(st["normed_one"], st["inverse_one"], grad_norm_one).astype(BF16)
        grad_conv_all.append(grad_conv.reshape(each, slab, grid_width, channels))
    grad_conv = jnp.concatenate(grad_conv_all, axis=0)
    back_before, back_after = halo_rows(grad_conv, "mp")
    halo_grad = jnp.concatenate([back_before, grad_conv, back_after], axis=1)
    padded_grad = jnp.pad(halo_grad, ((0, 0), (0, 0), (1, 1), (0, 0)))
    grad_conv_full = grad_conv.astype(F32)
    grad_first = jnp.concatenate([st["grad_first"] for st in state], axis=0).reshape(latents.shape)
    conv_back = jnp.zeros_like(grad_first)
    kernel_rows = []
    for down in range(3):
        for side in range(3):
            window_in = padded_in[:, down : down + slab, side : side + grid_width].astype(F32)
            kernel_rows.append(jnp.sum(window_in * grad_conv_full, axis=(0, 1, 2)))
            window_grad = padded_grad[
                :, 2 - down : 2 - down + slab, 2 - side : 2 - side + grid_width
            ].astype(F32)
            conv_back = conv_back + window_grad * kernel[down, side]
    kernel_rows.append(jnp.sum(grad_conv_full, axis=(0, 1, 2)))
    latents_grad = (grad_first + conv_back).astype(BF16)
    tail = jnp.stack(kernel_rows)
    taps = tail.shape[0]
    part = chunk // mp_size
    tail = jnp.transpose(tail.reshape(taps, dp_size, mp_size, part), (2, 1, 0, 3))
    tail = halve([tail.reshape(mp_size, dp_size * taps, part)], "mp", [0, 1], F32)
    tail = halve([tail.reshape(dp_size, taps, part)], "dp", dp_bits, F32)

    return (
        jnp.concatenate([st["result"] for st in state], axis=0).reshape(latents.shape),
        latents_grad,
        tail[: taps - 1].reshape(3, 3, part),
        tail[taps - 1],
        expand_sent,
        expand_small[0],
        expand_small[1],
        expand_small[2],
        shrink_sent.T,
        grad_shrink_bias,
        time_weight_grad,
        time_bias_grad,
        attention_sent[: clip // dp_size, 4 * width :],
        expand_small[5],
        attention_sent[:, : 3 * width].reshape(chunk, 3, width),
        expand_small[3],
        expand_small[4],
        attention_sent[:, 3 * width : 4 * width].T,
        grad_out_bias,
    )


def solution(mesh):
    return jax.shard_map(
        shards,
        mesh=mesh,
        in_specs=(
            P("dp", "mp", None, None),
            P(),
            P(),
            P(None, "mp"),
            P("mp"),
            P("mp"),
            P("mp"),
            P("mp", None),
            P(),
            P("dp", None),
            P(),
            P(),
            P("dp", None, None),
            P("dp"),
            P("dp"),
            P(None, "mp"),
            P("mp"),
            P(None, None, "mp"),
            P("mp"),
            P("mp"),
            P("mp", None),
            P(),
            P("dp", "mp", None, None),
        ),
        out_specs=(
            P("dp", "mp", None, None),
            P("dp", "mp", None, None),
            P(None, None, ("dp", "mp")),
            P(("dp", "mp")),
            P("dp", "mp"),
            P(("mp", "dp")),
            P(("mp", "dp")),
            P(("mp", "dp")),
            P("mp", "dp"),
            P("dp"),
            P(None, "dp"),
            P("dp"),
            P("dp", "mp"),
            P(("mp", "dp")),
            P("dp", None, "mp"),
            P(("mp", "dp")),
            P(("mp", "dp")),
            P("mp", "dp"),
            P("dp"),
        ),
        check_vma=False,
    )
```

```python
import functools
import math

import jax
import jax.numpy as jnp
from jax import lax
from jax.experimental import pallas as pl
from jax.experimental.pallas import tpu as pltpu
from jax.sharding import PartitionSpec as P

HEAD = 64
LANES = 128
F32 = jnp.float32
BF16 = jnp.bfloat16
SHRINK_CUT = 1152
EXPAND_CUT = 768


def swap(values, axis, mask):
    size = lax.axis_size(axis)
    return lax.ppermute(values, axis, [(i, i ^ mask) for i in range(size)])


def after(values, other):
    return lax.optimization_barrier((values, other))[0]


def halo_rows(shard, axis):
    size, length = (lax.axis_size(axis), shard.shape[1])
    up = [(i, i + 1) for i in range(size - 1)]
    down = [(j, i) for i, j in up]
    before = lax.ppermute(shard[:, length - 1 :], axis, up)
    after_rows = lax.ppermute(shard[:, :1], axis, down)
    return before, after_rows


def together(*values):
    return lax.optimization_barrier(values)


def sum_mp(values):
    values = values + swap(values, "mp", 1)
    return values + swap(values, "mp", 2)


def first_halves(grad, axis, bit):
    count = int(math.log2(lax.axis_size(axis)))
    grad = grad.reshape((2,) * count + grad.shape[1:])
    mine = (lax.axis_index(axis) >> bit) & 1
    pick = lambda side: lax.dynamic_index_in_dim(grad, side, count - 1 - bit, keepdims=False)
    return pick(1 - mine), pick(mine)


def halve(sent, kept, axis, bits, hold):
    count = int(math.log2(lax.axis_size(axis)))
    index = lax.axis_index(axis)
    left = list(range(count - 1, -1, -1))
    total, totals = (None, [])
    for turn, bit in enumerate(bits):
        place = left.index(bit)
        left.remove(bit)
        mine = (index >> bit) & 1
        if turn:
            pick = lambda side: lax.dynamic_index_in_dim(total, side, place, keepdims=False)
            sent, kept = pick(1 - mine).astype(BF16), pick(mine)
        got = swap(sent, axis, 1 << bit)
        if turn < len(hold):
            got = after(got, hold[turn])
        total = kept.astype(F32) + got.astype(F32)
        totals.append(total)
    return totals


def layer_norm(values):
    centred = values - jnp.mean(values, axis=-1, keepdims=True)
    inverse = lax.rsqrt(jnp.mean(centred * centred, axis=-1, keepdims=True) + 1e-06)
    return (centred * inverse, inverse)


def norm_back(normed, inverse, upstream):
    return inverse * (
        upstream
        - jnp.mean(upstream, axis=-1, keepdims=True)
        - normed * jnp.mean(upstream * normed, axis=-1, keepdims=True)
    )


def dot(spec, left, right):
    return jnp.einsum(spec, left, right, preferred_element_type=F32)


def attend_kernel(positions, lengths, q_ref, k_ref, v_ref, g_ref, o_ref, d_ref):
    item = pl.program_id(0)
    pair = pl.program_id(1)
    pairs = pl.num_programs(1)
    lanes = q_ref.shape[1]
    keys = k_ref.shape[0]
    limit = positions + lengths[item]
    lane = lax.broadcasted_iota(jnp.int32, (1, lanes), 1)
    scale = 1.0 / math.sqrt(HEAD)
    query = (q_ref[:positions].astype(F32) * scale).astype(BF16)
    key, value, grad = k_ref[...], v_ref[...], g_ref[...]
    tail = lax.broadcasted_iota(jnp.int32, (1, keys - positions), 1) + positions
    bias = jnp.concatenate([jnp.zeros((1, positions), F32), jnp.where(tail < limit, 0.0, -1e30)], axis=1)
    outs, d_queries, d_keys, d_values = [], [], [], []
    nt = (((1,), (1,)), ((), ()))
    for head in range(lanes // HEAD):
        here = (lane >= head * HEAD) & (lane < (head + 1) * HEAD)
        first = HEAD if head == 0 else 0
        query_head = jnp.where(here, query, jnp.zeros_like(query))
        value_ones = jnp.where(here, value, jnp.ones_like(value))
        scores = lax.dot_general(query_head, key, nt, preferred_element_type=F32) + bias
        peak = jnp.max(scores, axis=1, keepdims=True)
        weight = jnp.exp(scores - peak)
        weight_low = weight.astype(BF16)
        total = lax.dot_general(weight_low, value_ones, (((1,), (0,)), ((), ())), preferred_element_type=F32)
        inverse = 1.0 / total[:, first : first + 1]
        out = total * inverse
        outs.append(out)
        grad_head = jnp.where(here, grad, jnp.zeros_like(grad))
        dot = jnp.sum(grad_head.astype(F32) * out, axis=1, keepdims=True)
        dot_high = dot.astype(BF16)
        dot_low = (dot - dot_high.astype(F32)).astype(BF16)
        grad_ext = jnp.where(lane == first, -dot_high, jnp.where(lane == first + 1, -dot_low, grad_head))
        spread = lax.dot_general(grad_ext, value_ones, nt, preferred_element_type=F32)
        d_scores = (weight * spread).astype(BF16)
        d_query = lax.dot_general(d_scores, key, (((1,), (0,)), ((), ())), preferred_element_type=F32)
        d_queries.append(d_query * (inverse * scale))
        query_scaled = (query.astype(F32) * inverse).astype(BF16)
        grad_scaled = (grad.astype(F32) * inverse).astype(BF16)
        rows = slice(head * HEAD, (head + 1) * HEAD)
        d_keys.append(lax.dot_general(query_scaled.T[rows], d_scores, (((1,), (0,)), ((), ())), preferred_element_type=F32))
        d_values.append(lax.dot_general(grad_scaled.T[rows], weight_low, (((1,), (0,)), ((), ())), preferred_element_type=F32))
    low_half = lane < HEAD
    o_ref[...] = jnp.where(low_half, outs[0], outs[1]).astype(BF16)
    d_query = jnp.where(low_half, d_queries[0], d_queries[1]).astype(BF16)
    at = pl.multiple_of(pair * lanes, lanes)
    step = pairs * lanes
    d_ref[:positions, pl.ds(at, lanes)] = d_query
    d_ref[positions:, pl.ds(at, lanes)] = jnp.zeros((keys - positions, lanes), BF16)
    d_ref[:, pl.ds(at + step, lanes)] = jnp.concatenate(d_keys, axis=0).T.astype(BF16)
    d_ref[:, pl.ds(at + 2 * step, lanes)] = jnp.concatenate(d_values, axis=0).T.astype(BF16)


def attend(qkv, grad, lengths, positions):
    n, keys, w3 = qkv.shape
    w = w3 // 3
    pairs = w // 128
    spec = lambda off: pl.BlockSpec((None, keys, 128), lambda i, p, l: (i, 0, off * pairs + p))
    own = pl.BlockSpec((None, positions, 128), lambda i, p, l: (i, 0, p))
    return pl.pallas_call(
        functools.partial(attend_kernel, positions),
        out_shape=(jax.ShapeDtypeStruct((n, positions, w), BF16), jax.ShapeDtypeStruct((n, keys, w3), BF16)),
        grid_spec=pltpu.PrefetchScalarGridSpec(
            num_scalar_prefetch=1, grid=(n, pairs),
            in_specs=[spec(0), spec(1), spec(2), own],
            out_specs=[own, pl.BlockSpec((None, keys, w3), lambda i, p, l: (i, 0, 0))],
        ),
        compiler_params=pltpu.CompilerParams(vmem_limit_bytes=48 << 20),
        cost_estimate=pl.CostEstimate(flops=n * pairs * 2 * 12 * positions * keys * 128, bytes_accessed=n * keys * w * 14, transcendentals=n * pairs * 2 * positions * keys),
    )(lengths, qkv, qkv, qkv, grad)


def erf(x):
    x = jnp.clip(x, -3.832506856900711, 3.832506856900711)
    y = x * x
    a = [0.00022905065861350646, 0.0034082910107109506, 0.050955695062380861, 0.18520832239976145, 1.128379143519084]
    b = [-1.1791602954361697e-7, 0.000023547966471313185, 0.0010179625278914885, 0.014070470171167667, 0.11098505178285362, 0.49746925110067538, 1.0]
    p = a[0]
    for c in a[1:]: p = p * y + c
    q = b[0]
    for c in b[1:]: q = q * y + c
    return x * p / q


def expand_kernel(item_rows, x_ref, w_ref, b_ref, act_ref, slope_ref, sq_ref):
    items = x_ref.shape[0] // item_rows
    bias = b_ref[...].astype(F32)
    for i in range(items):
        rows = slice(i * item_rows, (i + 1) * item_rows)
        pre = jnp.dot(x_ref[rows], w_ref[...], preferred_element_type=F32) + bias
        cumulative = 0.5 * (1.0 + erf(pre * (1.0 / math.sqrt(2.0))))
        density = jnp.exp(-0.5 * pre * pre) * (1.0 / math.sqrt(2.0 * math.pi))
        act = pre * cumulative
        act_ref[rows] = act.astype(BF16)
        slope_ref[rows] = (cumulative + pre * density).astype(BF16)
        sq_ref[i] = jnp.sum(act * act, axis=0, keepdims=True)


def expand(x, w, b, item_rows, tile=256):
    rows, c = x.shape
    f = w.shape[1]
    items = rows // item_rows
    out = pl.BlockSpec((rows, tile), lambda j: (0, j))
    return pl.pallas_call(
        functools.partial(expand_kernel, item_rows),
        out_shape=(jax.ShapeDtypeStruct((rows, f), BF16), jax.ShapeDtypeStruct((rows, f), BF16), jax.ShapeDtypeStruct((items, 1, f), F32)),
        grid=(f // tile,),
        in_specs=[pl.BlockSpec((rows, c), lambda j: (0, 0)), pl.BlockSpec((c, tile), lambda j: (0, j)), pl.BlockSpec((1, tile), lambda j: (0, j))],
        out_specs=(out, out, pl.BlockSpec((items, 1, tile), lambda j: (0, 0, j))),
        compiler_params=pltpu.CompilerParams(vmem_limit_bytes=48 << 20),
        cost_estimate=pl.CostEstimate(flops=2 * rows * c * f, bytes_accessed=2 * (rows * c + c * f + 2 * rows * f), transcendentals=rows * f),
    )(x, w, b.reshape(1, f))


def shards(
    latents,
    depth_kernel,
    depth_bias,
    expand_weight,
    expand_bias,
    response_gain,
    response_bias,
    shrink_weight,
    shrink_bias,
    time_embed,
    time_weight,
    time_bias,
    caption,
    drop_flags,
    caption_lengths,
    text_weight,
    text_bias,
    project_weight,
    query_bias,
    value_bias,
    output_weight,
    output_bias,
    cotangent,
):
    items, slab, grid_width, channels = latents.shape
    dp_size, mp_size = lax.axis_size("dp"), lax.axis_size("mp")
    dp_bits = list(range(int(math.log2(dp_size))))
    dp_turned = dp_bits[1:] + dp_bits[:1]
    dp_index, mp_index = lax.axis_index("dp"), lax.axis_index("mp")
    rows = slab * grid_width
    positions = rows * mp_size
    hidden = expand_weight.shape[1]
    hidden_all = hidden * mp_size
    width = project_weight.shape[2]
    text_slots = caption.shape[1]
    text_rows = -(-text_slots // LANES) * LANES
    chunk = channels // dp_size

    def by_row(values):
        return values.reshape(items, rows, channels)

    def flat(values):
        return values.reshape(-1, values.shape[-1])

    kernel = depth_kernel.astype(F32)
    before, after_rows = halo_rows(latents, "mp")
    halo_in = jnp.concatenate([before, latents, after_rows], axis=1)
    padded_in = jnp.pad(halo_in, ((0, 0), (0, 0), (1, 1), (0, 0)))
    conv_out = depth_bias.astype(F32)
    for down in range(3):
        for side in range(3):
            conv_out = (
                conv_out
                + padded_in[:, down : down + slab, side : side + grid_width].astype(F32)
                * kernel[down, side]
            )
    normed_one, inverse_one = layer_norm(by_row(conv_out))
    normed_low = normed_one.astype(BF16)
    across = swap(normed_low, "mp", 2)
    core = swap(normed_low, "mp", 1)

    time_rows, caption_rows, project = lax.optimization_barrier(
        (time_embed, caption, project_weight, inverse_one)
    )[:3]
    modulation = jnp.dot(
        time_rows, time_weight.astype(F32), precision=lax.Precision.HIGHEST
    ) + time_bias.astype(F32)
    keep_text = (1 - drop_flags).astype(F32)
    text_in = jax.nn.silu(caption_rows.astype(F32) * keep_text[:, None, None]).astype(BF16)
    text_own = (dot("itk,kc->itc", text_in, text_weight) + text_bias.astype(F32)).astype(BF16)
    project = project.reshape(channels, 3 * width)
    project_bias = jnp.concatenate([query_bias, jnp.zeros_like(query_bias), value_bias]).astype(F32)
    across, core, project, text_own, modulation = together(across, core, project, text_own, modulation)
    scale = modulation[:, None, :channels]
    shift = modulation[:, None, channels:]
    diagonal = swap(across, "mp", 1)
    gathered_one = jnp.concatenate([normed_low, across, core, diagonal], axis=1)

    top, text_own = lax.optimization_barrier((by_row(cotangent), text_own, across))[:2]
    text_across = swap(text_own, "mp", 2)
    top_across = swap(top, "mp", 2)
    top_core, text_core = swap(top, "mp", 1), swap(text_own, "mp", 1)
    act, slope, squares = expand(flat(gathered_one), expand_weight, expand_bias, positions)
    squares, top_across, text_across = together(squares, top_across, text_across)
    act = act.reshape(items, positions, hidden)
    slope = slope.reshape(items, positions, hidden)
    top_diagonal, text_diagonal = swap(top_across, "mp", 1), swap(text_across, "mp", 1)

    gain = response_gain.astype(F32)
    col_norm = jnp.sqrt(squares[:, 0])
    denominator = sum_mp(jnp.sum(col_norm, axis=1)) / hidden_all + 1e-06
    ratio = (col_norm / denominator[:, None])[:, None, :]
    act_full = act.astype(F32)
    mixed = (gain * (act_full * ratio) + response_bias.astype(F32) + act_full).astype(BF16)
    shrink_part = dot("irf,fc->irc", mixed, shrink_weight).astype(BF16)

    def chip_sum(part):
        got = swap(part[:, 2 * rows : 4 * rows], "mp", 1)
        kept = part[:, : 2 * rows].astype(F32) + got.astype(F32)
        return kept[:, :rows], kept[:, rows:].astype(BF16)

    kept, sent = chip_sum(shrink_part)
    got = swap(sent, "mp", 2)
    top, top_across, top_core, top_diagonal, text_own, text_across, text_core, text_diagonal = (
        lax.optimization_barrier(
            (top, top_across, top_core, top_diagonal, text_own, text_across, text_core, text_diagonal, sent)
        )[:8]
    )
    grad_rows = jnp.concatenate([top, top_across, top_core, top_diagonal], axis=1)
    grad_att = dot("isc,dc->isd", grad_rows, output_weight).astype(BF16)
    pieces = (text_own, text_core, text_across, text_diagonal)
    text_full = jnp.concatenate(
        [lax.select_n(mp_index ^ holder, *pieces) for holder in range(mp_size)], axis=2
    )
    text_full = jnp.pad(text_full, ((0, 0), (0, text_rows - text_slots), (0, 0)))
    got, grad_att, text_full = together(got, grad_att, text_full)
    first_sum = by_row(latents).astype(F32) + kept + got.astype(F32) + shrink_bias.astype(F32)
    second_sum = first_sum * (1.0 + scale) + shift
    normed_two, inverse_two = layer_norm(second_sum)
    normed_low = normed_two.astype(BF16)
    across = swap(normed_low, "mp", 2)
    core = swap(normed_low, "mp", 1)
    diagonal = swap(across, "mp", 1)
    keys_in = jnp.concatenate([normed_low, across, core, diagonal, text_full], axis=1)

    qkv = (dot("isc,cd->isd", keys_in, project) + project_bias).astype(BF16)
    attended, grad_qkv = attend(qkv, grad_att, caption_lengths, positions)
    grad_keys = dot("isd,cd->isc", grad_qkv, project).astype(BF16)
    kept, sent = chip_sum(grad_keys)
    got = swap(sent, "mp", 2)

    grad_qkv_late, attended_late = lax.optimization_barrier((grad_qkv, attended, sent))[:2]
    project_grads = dot("rc,rd->cd", flat(keys_in), flat(grad_qkv_late)).astype(BF16)
    output_grads = dot("rc,rd->cd", flat(grad_rows), flat(attended_late)).astype(BF16)
    out_part = dot("isd,dc->isc", attended_late, output_weight).astype(BF16)

    def halves(grads, at):
        grads = [grad.reshape(dp_size, -1, grad.shape[-1]) for grad in grads]
        parts = []
        for low, high, bit in ((0, at, dp_bits[0]), (at, None, dp_turned[0])):
            picked, start = ([], 0)
            for grad in grads:
                size = grad.shape[-1]
                stop = size if high is None else min(size, high - start)
                first = max(0, low - start)
                if stop > first:
                    picked.append(first_halves(grad[:, :, first:stop], "dp", bit))
                start += size
            parts += [jnp.concatenate(pair, axis=-1) if len(pair) > 1 else pair[0] for pair in zip(*picked)]
        return parts

    got, out_part, *attention_parts = together(
        got, out_part, *halves([project_grads, output_grads], 2 * width)
    )
    grad_top = by_row(cotangent).astype(F32)
    grad_norm_two = kept + got.astype(F32)
    grad_second = grad_top + norm_back(normed_two, inverse_two, grad_norm_two)
    grad_first = grad_second * (1.0 + scale)
    first_low = grad_first.astype(BF16)
    across = swap(first_low, "mp", 2)
    core = swap(first_low, "mp", 1)

    late_top, late_first, late_second, late_sum = lax.optimization_barrier(
        (grad_top, grad_first, grad_second, first_sum, first_low)
    )[:4]
    grad_modul = jnp.concatenate(
        [jnp.sum(late_second * late_sum, axis=1), jnp.sum(late_second, axis=1)], axis=1
    )
    grad_out_bias = jnp.sum(late_top, axis=(0, 1))
    grad_shrink_bias = jnp.sum(late_first, axis=(0, 1))
    across, grad_modul, grad_out_bias, grad_shrink_bias = together(
        across, grad_modul, grad_out_bias, grad_shrink_bias
    )
    diagonal = swap(across, "mp", 1)
    first_rows = jnp.concatenate([first_low, across, core, diagonal], axis=1)

    columns = after(grad_keys[:, positions : positions + text_slots], across)
    columns = [columns[:, :, i * width : (i + 1) * width] for i in range(mp_size)]

    def columns_of(holder):
        return lax.select_n(holder, *columns)

    text_sent = jnp.stack([columns_of(mp_index ^ 1), columns_of(mp_index ^ 3)])
    text_kept = jnp.stack([columns_of(mp_index), columns_of(mp_index ^ 2)])
    text_kept = text_kept.astype(F32) + swap(text_sent, "mp", 1).astype(F32)
    text_got = swap(text_kept[1].astype(BF16), "mp", 2)

    grad_mixed = dot("irc,fc->irf", first_rows, shrink_weight)
    weighted = jnp.sum(grad_mixed * act_full, axis=1)
    grad_response_bias = jnp.sum(grad_mixed, axis=(0, 1))
    grad_mixed = grad_mixed.astype(BF16)
    grad_ratio = gain * weighted
    cross_part = jnp.sum(grad_ratio * col_norm, axis=1)
    cross = sum_mp(cross_part)
    late_rows, text_got = lax.optimization_barrier((first_rows, text_got, cross_part))[:2]
    grad_text = (text_kept[0] + text_got.astype(F32)).astype(BF16)
    text_grads = dot("itk,itc->kc", text_in, grad_text).astype(BF16)
    grad_text_bias = jnp.sum(grad_text.astype(F32), axis=(0, 1))
    shrink_grads = dot("rc,rf->cf", flat(late_rows), flat(mixed)).astype(BF16)
    clip = text_weight.shape[0] // dp_size
    text_pad = jnp.pad(text_grads.reshape(dp_size, clip, width), ((0, 0), (0, chunk - clip), (0, 0)))
    cross, *shrink_parts = together(cross, *halves([shrink_grads, text_pad], SHRINK_CUT))
    grad_col = (
        grad_ratio / denominator[:, None]
        - (cross / (hidden_all * denominator * denominator))[:, None]
    )
    grad_act = (
        grad_mixed.astype(F32) * (gain * ratio + 1.0)
        + (grad_col / col_norm)[:, None, :] * act_full
    )
    grad_pre = (grad_act * slope.astype(F32)).astype(BF16)

    out_kept, out_sent = chip_sum(after(out_part, cross))
    out_got = swap(out_sent, "mp", 2)

    expand_grads = dot("rc,rf->cf", flat(gathered_one), flat(grad_pre)).astype(BF16)
    grad_pre_late, *expand_parts = together(grad_pre, *halves([expand_grads], EXPAND_CUT))
    grad_norm_part = dot("irf,cf->irc", grad_pre_late, expand_weight).astype(BF16)
    kept, sent = chip_sum(grad_norm_part)
    got = swap(sent, "mp", 2)
    grad_qkv_sum = jnp.sum(flat(after(grad_qkv, sent)).astype(F32), axis=0)
    grad_pre_sum = jnp.sum(flat(after(grad_pre, sent)).astype(F32), axis=0)
    weighted_late, grad_response_bias = lax.optimization_barrier((weighted, grad_response_bias, sent))[:2]
    grad_gain = jnp.sum(weighted_late * ratio[:, 0], axis=0)
    out_got = after(out_got, sent)
    result = (second_sum + out_kept + out_got.astype(F32) + output_bias.astype(F32)).astype(BF16)
    got, result = together(got, result)
    grad_norm_one = kept + got.astype(F32)
    grad_conv = norm_back(normed_one, inverse_one, grad_norm_one).astype(BF16)
    grad_conv = grad_conv.reshape(latents.shape)
    back_before, back_after = halo_rows(grad_conv, "mp")
    grad_conv_full = grad_conv.astype(F32)
    kernel_rows = []
    for down in range(3):
        for side in range(3):
            window_in = padded_in[:, down : down + slab, side : side + grid_width].astype(F32)
            kernel_rows.append(jnp.sum(window_in * grad_conv_full, axis=(0, 1, 2)))
    kernel_rows.append(jnp.sum(grad_conv_full, axis=(0, 1, 2)))

    halo_grad = jnp.concatenate([back_before, grad_conv, back_after], axis=1)
    padded_grad = jnp.pad(halo_grad, ((0, 0), (0, 0), (1, 1), (0, 0)))
    conv_back = jnp.zeros(latents.shape, F32)
    for down in range(3):
        for side in range(3):
            window_grad = padded_grad[
                :, 2 - down : 2 - down + slab, 2 - side : 2 - side + grid_width
            ].astype(F32)
            conv_back = conv_back + window_grad * kernel[down, side]
    latents_grad = (grad_first.reshape(latents.shape) + conv_back).astype(BF16)

    attention_a = halve(*attention_parts[:2], "dp", dp_bits, [first_rows, weighted, sent])[-1]
    attention_b = halve(*attention_parts[2:], "dp", dp_turned, [first_rows, grad_pre, sent])[-1]
    attention_sent = jnp.concatenate([attention_a, attention_b], axis=1)
    small = jnp.stack(
        [*kernel_rows, grad_out_bias, grad_shrink_bias, grad_pre_sum, grad_gain, grad_response_bias]
    )
    shrink_a = halve(*shrink_parts[:2], "dp", dp_bits, [sent, small, latents_grad])[-1]
    shrink_b = halve(*shrink_parts[2:], "dp", dp_turned, [sent, small, latents_grad])[-1]
    expand_a = halve(*expand_parts[:2], "dp", dp_bits, [small, latents_grad])
    expand_b = halve(*expand_parts[2:], "dp", dp_turned, [small, latents_grad])
    text_weight_sent = shrink_b[:clip, hidden - SHRINK_CUT :]
    shrink_sent = jnp.concatenate([shrink_a, shrink_b[:, : hidden - SHRINK_CUT]], axis=1)
    expand_sent = jnp.concatenate([expand_a[-1], expand_b[-1]], axis=1)
    late = (expand_a[-2:][0], expand_b[-2:][0])

    grad_modul = sum_mp(after(grad_modul, small))
    embeds = time_embed
    for bit in reversed(dp_bits):
        wide = grad_modul.shape[1] // 2
        mine = (dp_index >> bit) & 1
        out = lax.dynamic_slice_in_dim(grad_modul, (1 - mine) * wide, wide, axis=1)
        stay = lax.dynamic_slice_in_dim(grad_modul, mine * wide, wide, axis=1)
        came = after(swap(jnp.concatenate([out, embeds], axis=1), "dp", 1 << bit), late)
        grad_modul = jnp.concatenate([stay, came[:, :wide]], axis=0)
        embeds = jnp.concatenate([embeds, came[:, wide:]], axis=0)
    time_weight_grad = jnp.dot(embeds.T, grad_modul, precision=lax.Precision.HIGHEST)
    time_bias_grad = jnp.sum(grad_modul, axis=0)

    spare = jnp.zeros((hidden - 3 * width,), F32)
    mixture = jnp.concatenate(
        [grad_qkv_sum[:width], grad_qkv_sum[2 * width :], grad_text_bias, spare]
    )
    small = jnp.concatenate([small, mixture[None]], axis=0)
    for bit in dp_bits:
        small = small + after(swap(small, "dp", 1 << bit), late)
    taps = len(kernel_rows)
    shared = sum_mp(small[: taps + 2])
    part = chunk // mp_size
    tail = lax.dynamic_slice_in_dim(shared[:taps], (dp_index * mp_size + mp_index) * part, part, axis=1)
    own = lax.dynamic_slice_in_dim(
        jnp.concatenate([shared[taps:], small[taps + 2 : taps + 5]]), dp_index * chunk, chunk, axis=1
    )
    thirds = small[taps + 5, : 3 * width].reshape(3, width)
    thirds = lax.dynamic_slice_in_dim(thirds, dp_index * part, part, axis=1)

    return (
        result.reshape(latents.shape),
        latents_grad,
        tail[: taps - 1].reshape(3, 3, part),
        tail[taps - 1],
        expand_sent,
        own[2],
        own[3],
        own[4],
        shrink_sent.T,
        own[1],
        time_weight_grad,
        time_bias_grad,
        text_weight_sent,
        thirds[2],
        attention_sent[:, : 3 * width].reshape(chunk, 3, width),
        thirds[0],
        thirds[1],
        attention_sent[:, 3 * width :].T,
        own[0],
    )


def solution(mesh):
    return jax.shard_map(
        shards,
        mesh=mesh,
        in_specs=(
            P("dp", "mp", None, None),
            P(),
            P(),
            P(None, "mp"),
            P("mp"),
            P("mp"),
            P("mp"),
            P("mp", None),
            P(),
            P("dp", None),
            P(),
            P(),
            P("dp", None, None),
            P("dp"),
            P("dp"),
            P(None, "mp"),
            P("mp"),
            P(None, None, "mp"),
            P("mp"),
            P("mp"),
            P("mp", None),
            P(),
            P("dp", "mp", None, None),
        ),
        out_specs=(
            P("dp", "mp", None, None),
            P("dp", "mp", None, None),
            P(None, None, ("dp", "mp")),
            P(("dp", "mp")),
            P("dp", "mp"),
            P(("mp", "dp")),
            P(("mp", "dp")),
            P(("mp", "dp")),
            P("mp", "dp"),
            P("dp"),
            P(None, "dp"),
            P("dp"),
            P("dp", "mp"),
            P(("mp", "dp")),
            P("dp", None, "mp"),
            P(("mp", "dp")),
            P(("mp", "dp")),
            P("mp", "dp"),
            P("dp"),
        ),
        check_vma=False,
    )
```
